256 devices in a mesh: pts: 128 (over z, y, x), slab: 2 (over core).
Axes of the slice: x: 4, y: 4, z: 8, core: 2. Of those that a mesh axis runs over, the one named last changes fastest.
Arguments:
- features: float32 [65536, 256], P(('slab', 'pts')), parts along dimension 0, may hold values from -25 to 25
- orders: int32 [2, 65536], P(None, ('slab', 'pts')), parts along dimension 1, may hold values from 0 to 32767, as said below
- norm_gains: float32 [2, 2, 256], replicated, may hold values from 0.1 to 1.9
- qkv_weight: bfloat16 [2, 256, 768], replicated, may hold values from -4 to 4
- proj_weight: bfloat16 [2, 256, 256], replicated, may hold values from -0.375 to 0.375
- fc1_weight: bfloat16 [2, 256, 1024], replicated, may hold values from -0.375 to 0.375
- fc2_weight: bfloat16 [2, 1024, 256], replicated, may hold values from -0.1875 to 0.1875
Outputs:
- output_features: float32 [65536, 256], P(('slab', 'pts')), parts along dimension 0
The draws below stay inside these ranges and needn't reach their ends.
There are 2 independent parts, one for each index of `slab`. The reference program is written for one: setup_inputs(seed, part) draws one part's arguments, and reference() takes and returns one part's arrays. A program takes and returns all parts, laid end to end along the dimension named above; an argument that names none is the same for every part. Nothing has to cross between parts.
Inputs may be any that keep to these rules, and one draw needn't show every extreme that they name: `orders`: each row is a permutation of the 32768 storage rows. In each row the 256 serial positions of one device take exactly 1 or 3 of their points from the rows stored on each device, 3 from half of the devices.
All inputs are finite; a program needn't handle non-finite values.
Results may differ from the reference program's by a relative error of at most 0.013.
Values may be sent and summed in bfloat16 or wider, within the bound.
A program may use at most 64 MiB of HBM per device.

```python
import jax
import jax.numpy as jnp
from jax import lax

C = 256
HEADS = 16
FFN_WIDTH = 1024
PATCH = 1024
BLOCKS = 2
PDEV = 256
NPTS = 32768


def draw_features(key, part):
    first = jax.random.fold_in(jax.random.fold_in(key, 11), 0)
    base_rows = jax.random.normal(first, (NPTS, C), jnp.float32)
    return jnp.clip(base_rows, -25.0, 25.0)


def draw_qkv_weight(key, part):
    base_weight = jax.random.normal(jax.random.fold_in(key, 23), (BLOCKS, C, 3 * C), jnp.float32) * C ** (-0.5)
    return jnp.clip(base_weight, -4.0, 4.0).astype(jnp.bfloat16)


def one_order(order_key):
    peers = NPTS // PDEV
    base_load = PDEV // (2 * peers)
    extra_load = PDEV // peers
    key_heavy, key_shuffle, key_final = jax.random.split(order_key, 3)
    heavy = (jax.random.permutation(key_heavy, peers) < peers // 2).astype(jnp.int32)
    dest_ids = jnp.arange(peers, dtype=jnp.int32)[:, None]
    source_ids = jnp.arange(peers, dtype=jnp.int32)[None, :]
    loads = base_load + extra_load * heavy[(source_ids - dest_ids) % peers]
    before = jnp.cumsum(loads, axis=0) - loads
    row_end = jnp.cumsum(loads, axis=1)
    slot_ids = jnp.arange(PDEV, dtype=jnp.int32)
    sources = jax.vmap(lambda ends: jnp.searchsorted(ends, slot_ids, side='right'))(row_end).astype(jnp.int32)
    dest_grid = jnp.broadcast_to(dest_ids, (peers, PDEV))
    start_in_row = row_end[dest_grid, sources] - loads[dest_grid, sources]
    ranks = before[dest_grid, sources] + slot_ids[None, :] - start_in_row
    shuffles = jax.vmap(lambda sub_key: jax.random.permutation(sub_key, PDEV))(jax.random.split(key_shuffle, peers)).astype(jnp.int32)
    storage_rows = sources * PDEV + shuffles[sources, ranks]
    finals = jax.vmap(lambda sub_key: jax.random.permutation(sub_key, PDEV))(jax.random.split(key_final, peers)).astype(jnp.int32)
    placed = jnp.take_along_axis(storage_rows, finals, axis=1)
    return placed.reshape(NPTS).astype(jnp.int32)


def draw_orders(key, part):
    block_keys = jax.random.split(jax.random.fold_in(key, 37), BLOCKS)
    return jax.vmap(one_order)(block_keys).astype(jnp.int32)


def scatter_about(key, dims, scale, most, held_as=jnp.bfloat16):
    entries = jax.random.normal(key, dims, jnp.float32) * scale
    return jnp.minimum(jnp.maximum(entries, -most), most).astype(held_as)


def setup_inputs(seed: int = 0, part: int = 0) -> dict:
    key_of = jax.random.split(jax.random.key(seed), 8)
    part_keys = jax.random.split(jax.random.fold_in(key_of[7], part), 8)
    return {
        "features": draw_features(jax.random.fold_in(jax.random.fold_in(key_of[7], part), 71), part),
        "orders": draw_orders(jax.random.fold_in(jax.random.fold_in(key_of[7], part), 71), part),
        "norm_gains": jnp.clip(1.0 + 0.18 * jax.random.normal(key_of[2], (BLOCKS, 2, C), jnp.float32), 0.1, 1.9),
        "qkv_weight": draw_qkv_weight(jax.random.fold_in(key_of[7], 71), part),
        "proj_weight": scatter_about(key_of[4], (BLOCKS, C, C), C ** -0.5, 0.375),
        "fc1_weight": scatter_about(key_of[5], (BLOCKS, C, FFN_WIDTH), C ** -0.5, 0.375),
        "fc2_weight": scatter_about(key_of[6], (BLOCKS, FFN_WIDTH, C), FFN_WIDTH ** -0.5, 0.1875),
    }


def layer_norm(values, gain_row):
    center = values - lax.optimization_barrier(jnp.mean(values, axis=1, keepdims=True))
    spread = lax.optimization_barrier(jnp.mean(center * center, axis=1, keepdims=True))
    return center * lax.rsqrt(spread + 1e-05) * gain_row

def reference(features, orders, norm_gains, qkv_weight, proj_weight, fc1_weight, fc2_weight):
    state_rows = features
    head_size = C // HEADS
    score_scale = head_size ** (-0.5)
    for block_index in range(BLOCKS):
        order_row = orders[block_index].astype(jnp.int32)
        serial = state_rows[order_row]
        normed = layer_norm(serial, norm_gains[block_index, 0]).astype(jnp.bfloat16)
        projected_all = jnp.dot(normed, qkv_weight[block_index], preferred_element_type=jnp.float32).astype(jnp.bfloat16)
        shaped = projected_all.astype(jnp.float32).reshape(NPTS // PATCH, PATCH, 3, HEADS, head_size)

        def one_patch(patch_rows):
            scores = jnp.einsum('qhd,khd->hqk', patch_rows[:, 0], patch_rows[:, 1]) * score_scale
            row_peak = lax.optimization_barrier(jnp.max(scores, axis=2, keepdims=True))
            weights = jnp.exp(scores - row_peak)
            probabilities = (weights / lax.optimization_barrier(jnp.sum(weights, axis=2, keepdims=True))).astype(jnp.bfloat16)
            probabilities = lax.optimization_barrier(probabilities).astype(jnp.float32)
            return jnp.einsum('hqk,khd->qhd', probabilities, patch_rows[:, 2])
        mixed_heads = lax.map(one_patch, shaped).reshape(NPTS, C).astype(jnp.bfloat16)
        attended = serial + jnp.dot(mixed_heads, proj_weight[block_index], preferred_element_type=jnp.float32)
        normed_two = layer_norm(attended, norm_gains[block_index, 1]).astype(jnp.bfloat16)
        expanded = jax.nn.gelu(jnp.dot(normed_two, fc1_weight[block_index], preferred_element_type=jnp.float32), approximate=False).astype(jnp.bfloat16)
        updated = attended + jnp.dot(expanded, fc2_weight[block_index], preferred_element_type=jnp.float32)
        state_rows = jnp.zeros_like(state_rows).at[order_row].set(updated)
    return state_rows
```

```python
import functools
import math

import jax
import jax.numpy as jnp
from jax import lax
from jax.experimental import pallas as pl
from jax.experimental.pallas import tpu as pltpu
from jax.sharding import PartitionSpec as P

HEADS = 16
PATCH = 1024
HALF = 128
SLOTS = 3
F32 = jnp.float32
BF16 = jnp.bfloat16
MESH = pl.DeviceIdType.MESH


def offsets(sizes):
    nz, ny, nx = sizes
    every = [(a, b, c) for a in range(nz) for b in range(ny) for c in range(nx)]

    def hops(o):
        return sum(min(v, n - v) for v, n in zip(o, sizes))

    return sorted((o for o in every if o != (0, 0, 0)), key=lambda o: (-hops(o), o[1], o[2], o[0]))


def iota(shape, dim):
    return lax.broadcasted_iota(jnp.int32, shape, dim)


def one_hot(cond):
    return jnp.where(cond, 1.0, 0.0).astype(BF16)


def mm(a, b):
    return jnp.dot(a, b, preferred_element_type=F32)


def layer_norm(values, gain_row):
    center = values - jnp.mean(values, axis=1, keepdims=True)
    spread = jnp.mean(center * center, axis=1, keepdims=True)
    return center * lax.rsqrt(spread + 1e-05) * gain_row


def stack_halves(rows):
    return jnp.concatenate((rows[:, :HALF], rows[:, HALF:]), axis=0)


def join_halves(stacked):
    count = stacked.shape[0] // 2
    return jnp.concatenate((stacked[:count], stacked[count:]), axis=1)


def kernel(
    sizes, feat_hbm, orders_hbm, gains_hbm, qkv_hbm, proj_hbm, fc1_hbm, fc2_hbm, out_ref,
    feat, orders, gains, qkv_w, proj_w, fc1_w, fc2_w,
    req_send, req_recv, row_send, row_recv, near,
    pick_in, pick_back, pick_out, pick_home, spread, q_buf, k_buf, v_buf, mixed,
    load_sem, self_sem, req_ssem, req_rsem, row_ssem, row_rsem, near_ssem, near_rsem,
):
    nz, ny, nx = sizes
    peers = nz * ny * nx
    rows = feat.shape[0]
    width = 2 * HALF
    slots = SLOTS * peers
    blocks = orders.shape[0]
    me = lax.axis_index("pts")
    zs = [jnp.bitwise_and(jnp.right_shift(me, 4) + i, nz - 1) * (ny * nx) for i in range(nz)]
    ys = [jnp.bitwise_and(jnp.right_shift(me, 2) + i, ny - 1) * nx for i in range(ny)]
    xs = [jnp.bitwise_and(me + i, nx - 1) for i in range(nx)]
    order = offsets(sizes)

    barrier = pltpu.get_barrier_semaphore()

    def greet(step, carry):
        other = jnp.bitwise_and(me + step, peers - 1)
        pl.semaphore_signal(barrier, inc=1, device_id={"pts": other}, device_id_type=MESH)
        return carry

    lax.fori_loop(1, peers, greet, 0)

    loads = [
        pltpu.make_async_copy(src, dst, load_sem.at[i])
        for i, (src, dst) in enumerate(
            (
                (orders_hbm, orders), (feat_hbm, feat), (gains_hbm, gains), (qkv_hbm, qkv_w),
                (proj_hbm, proj_w), (fc1_hbm, fc1_w), (fc2_hbm, fc2_w),
            )
        )
    ]
    for load in loads:
        load.start()
    loads[0].wait()

    ri = iota((rows, rows), 0)
    ci = iota((rows, rows), 1)
    keys = []
    left, right = [], []
    for b in range(blocks):
        order_row = orders[b : b + 1, :]
        owner_row = jnp.right_shift(order_row, 8).astype(F32)
        within_row = jnp.bitwise_and(order_row, rows - 1).astype(F32)
        owner_col = jnp.sum(jnp.where(ri == ci, owner_row, 0.0), axis=1, keepdims=True)
        within_col = jnp.sum(jnp.where(ri == ci, within_row, 0.0), axis=1, keepdims=True)
        same = owner_col == owner_row
        rank_col = jnp.sum(jnp.where(same & (ci < ri), 1.0, 0.0), axis=1, keepdims=True)
        rank_row = jnp.sum(jnp.where(same & (ri < ci), 1.0, 0.0), axis=0, keepdims=True)
        keys.append(
            (
                (2.0 * (rank_row * peers + owner_row)).astype(jnp.int32),
                (2.0 * (rank_col * peers + owner_col)).astype(jnp.int32),
            )
        )
        left.append(one_hot(ri == (2.0 * owner_row + b).astype(jnp.int32)))
        lane = iota((rows, HALF), 1)
        right.append(
            jnp.where(rank_col.astype(jnp.int32) == lane, within_col + 1.0, 0.0).astype(BF16)
        )
    request = mm(jnp.concatenate(left, axis=1), jnp.concatenate(right, axis=0))
    req_send.reshape(2 * peers, HALF)[...] = request.astype(BF16)

    pl.semaphore_wait(barrier, peers - 1)

    def to_all(src, dst, ssem, rsem, mine):
        own = pltpu.make_async_copy(src(me), dst(me), mine)
        own.start()
        for a, b, c in order:
            other = zs[a] + ys[b] + xs[c]
            pltpu.make_async_remote_copy(
                src_ref=src(other), dst_ref=dst(me), send_sem=ssem, recv_sem=rsem,
                device_id={"pts": other}, device_id_type=MESH,
            ).start()
        return own

    def all_of(ref, sem):
        pltpu.make_async_copy(ref, ref, sem).wait()

    own = to_all(lambda i: req_send.at[i], lambda i: req_recv.at[i], req_ssem, req_rsem, self_sem.at[0])

    for b in range(blocks):
        key_row, key_col = keys[b]
        for half in range(2):
            part = pl.ds(half * rows, rows)
            pick_in[b, part, :] = one_hot(iota((rows, 2 * slots), 1) == key_col + half)
            pick_back[b, :, part] = one_hot(iota((2 * slots, rows), 0) == key_row + half)
        spread[b] = one_hot(ri - jnp.bitwise_and(ri, 1) + b == ci)
    for load in loads[1:]:
        load.wait()

    own.wait()
    all_of(req_recv.at[pl.ds(0, peers - 1)], req_rsem)
    asked = req_recv.reshape(2 * peers, HALF)[...]

    def selections(b):
        wanted = mm(spread[b], asked)
        parity = jnp.bitwise_and(iota(wanted.shape, 0), 1).astype(F32)
        wanted = jnp.where(wanted > 0.5, wanted - 1.0 + rows * parity, -4.0)
        return wanted

    def fill_out(b, wanted):
        for j in range(SLOTS):
            col = wanted[:, j : j + 1].astype(jnp.int32)
            pick_out[b, pl.ds(j * 2 * peers, 2 * peers), :] = one_hot(iota((2 * peers, 2 * rows), 1) == col)

    def fill_home(b, wanted):
        flat = wanted.T.astype(jnp.int32)
        for j in range(SLOTS):
            pick_home[b, :, pl.ds(j * 2 * peers, 2 * peers)] = one_hot(
                iota((2 * rows, 2 * peers), 0) == flat[j : j + 1, :]
            )

    def ship(phase, values):
        row_send.at[phase].reshape(2 * slots, HALF)[...] = values.astype(BF16)
        return to_all(
            lambda i: row_send.at[phase, :, i], lambda i: row_recv.at[phase, :, i],
            row_ssem.at[phase], row_rsem.at[phase], self_sem.at[1 + phase],
        )

    def landed(phase, own):
        own.wait()
        all_of(row_recv.at[phase, :, pl.ds(0, peers - 1)], row_rsem.at[phase])
        return row_recv.at[phase].reshape(2 * slots, HALF)[...]

    wanted0 = selections(0)
    fill_out(0, wanted0)
    own = ship(0, mm(pick_out[0], stack_halves(feat[...].astype(BF16))))

    fill_home(0, wanted0)
    wanted1 = selections(1)
    fill_out(1, wanted1)
    fill_home(1, wanted1)

    scale = (width // HEADS) ** (-0.5) * math.log2(math.e)
    near_copies = []
    for b in range(blocks):
        serial = join_halves(mm(pick_in[b], landed(2 * b, own)))
        normed = layer_norm(serial, gains[b, 0:1, :]).astype(BF16)
        near[b, 0] = normed
        copies = []
        for o in (2, 1, 3):
            copy = pltpu.make_async_remote_copy(
                src_ref=near.at[b, 0], dst_ref=near.at[b, o], send_sem=near_ssem.at[b, o],
                recv_sem=near_rsem.at[b, o], device_id={"pts": me - xs[0] + xs[o]}, device_id_type=MESH,
            )
            copy.start()
            copies.append(copy)
        near_copies += copies

        projected = mm(normed, qkv_w[b])
        q_buf[...] = (projected[:, :width] * scale).astype(BF16)

        def keep(at, pair):
            k_buf[pl.ds(at * rows, rows), :] = pair[:, :width].astype(BF16)
            values = pair[:, width:].astype(BF16)
            ones = jnp.ones((rows, HALF), BF16)
            for half in range(2):
                v_buf[half, pl.ds(at * rows, rows), :] = jnp.concatenate(
                    (values[:, half * HALF : (half + 1) * HALF], ones), axis=1
                )

        keep(0, projected[:, width:])
        for o, copy in zip((2, 1, 3), copies):
            copy.wait_recv()
        for o in (1, 2, 3):
            keep(o, mm(near[b, o], qkv_w[b, :, width:]))

        def head(h, carry):
            group = h // (HEADS // 2)
            within = h % (HEADS // 2)
            mask = one_hot(jnp.right_shift(iota((1, width), 1), 4) == h)
            scores = lax.dot_general(
                q_buf[...] * mask, k_buf[...], (((1,), (1,)), ((), ())), preferred_element_type=F32
            )
            peak = jnp.max(scores, axis=1, keepdims=True)
            weights = jnp.exp2(scores - peak).astype(BF16)
            both = mm(weights, v_buf[group])
            result = both[:, :HALF] / both[:, HALF:]
            mine = jnp.right_shift(iota((rows, HALF), 1), 4) == within
            mixed[group] = jnp.where(mine, result, mixed[group])
            return carry

        lax.fori_loop(0, HEADS, head, 0, unroll=2)
        heads = jnp.concatenate((mixed[0], mixed[1]), axis=1).astype(BF16)
        attended = serial + mm(heads, proj_w[b])
        normed_two = layer_norm(attended, gains[b, 1:2, :]).astype(BF16)
        hidden = mm(normed_two, fc1_w[b])
        expanded = (0.5 * hidden * (1.0 + lax.erf(hidden * (0.5**0.5)))).astype(BF16)
        updated = attended + mm(expanded, fc2_w[b])

        own = ship(2 * b + 1, mm(pick_back[b], stack_halves(updated.astype(BF16))))
        state = mm(pick_home[b], landed(2 * b + 1, own))
        if b + 1 < blocks:
            own = ship(2 * b + 2, mm(pick_out[b + 1], state.astype(BF16)))
        else:
            out_ref[...] = join_halves(state)

    all_of(req_send.at[pl.ds(0, peers - 1)], req_ssem)
    for phase in range(2 * blocks):
        all_of(row_send.at[phase, :, pl.ds(0, peers - 1)], row_ssem.at[phase])
    for copy in near_copies:
        copy.wait_send()


def local(sizes, features, orders, norm_gains, qkv_weight, proj_weight, fc1_weight, fc2_weight):
    rows, width = features.shape
    peers = math.prod(sizes)
    blocks = orders.shape[0]
    args = (features, orders, norm_gains, qkv_weight, proj_weight, fc1_weight, fc2_weight)
    slots = SLOTS * peers
    return pl.pallas_call(
        functools.partial(kernel, sizes),
        out_shape=jax.ShapeDtypeStruct((rows, width), F32),
        in_specs=[pl.BlockSpec(memory_space=pl.ANY)] * len(args),
        out_specs=pl.BlockSpec(memory_space=pltpu.VMEM),
        scratch_shapes=[pltpu.VMEM(a.shape, a.dtype) for a in args]
        + [
            pltpu.VMEM((peers, 2, HALF), BF16),
            pltpu.VMEM((peers, 2, HALF), BF16),
            pltpu.VMEM((2 * blocks, SLOTS, peers, 2, HALF), BF16),
            pltpu.VMEM((2 * blocks, SLOTS, peers, 2, HALF), BF16),
            pltpu.VMEM((blocks, PATCH // rows, rows, width), BF16),
            pltpu.VMEM((blocks, 2 * rows, 2 * slots), BF16),
            pltpu.VMEM((blocks, 2 * slots, 2 * rows), BF16),
            pltpu.VMEM((blocks, 2 * slots, 2 * rows), BF16),
            pltpu.VMEM((blocks, 2 * rows, 2 * slots), BF16),
            pltpu.VMEM((blocks, rows, rows), BF16),
            pltpu.VMEM((rows, width), BF16),
            pltpu.VMEM((PATCH, width), BF16),
            pltpu.VMEM((2, PATCH, width), BF16),
            pltpu.VMEM((2, rows, HALF), F32),
            pltpu.SemaphoreType.DMA((len(args),)),
            pltpu.SemaphoreType.DMA((1 + 2 * blocks,)),
            pltpu.SemaphoreType.DMA,
            pltpu.SemaphoreType.DMA,
            pltpu.SemaphoreType.DMA((2 * blocks,)),
            pltpu.SemaphoreType.DMA((2 * blocks,)),
            pltpu.SemaphoreType.DMA((blocks, 4)),
            pltpu.SemaphoreType.DMA((blocks, 4)),
        ],
        compiler_params=pltpu.CompilerParams(collective_id=0, has_side_effects=True),
    )(*args)


def solution(mesh):
    sizes = (8, 4, 4)
    placed = (P(("slab", "pts"), None), P(None, ("slab", "pts")), P(), P(), P(), P(), P())
    return jax.shard_map(
        functools.partial(local, sizes),
        mesh=mesh,
        in_specs=placed,
        out_specs=P(("slab", "pts"), None),
        check_vma=False,
    )
```

```python
import functools
import math

import jax
import jax.numpy as jnp
from jax import lax
from jax.experimental import pallas as pl
from jax.experimental.pallas import tpu as pltpu
from jax.sharding import PartitionSpec as P

HEADS = 16
PATCH = 1024
HALF = 128
GROUP = 2
UNROLL = 8
SLOTS = 3
F32 = jnp.float32
BF16 = jnp.bfloat16
MESH = pl.DeviceIdType.MESH


def offsets(sizes):
    nz, ny, nx = sizes
    every = [(a, b, c) for a in range(nz) for b in range(ny) for c in range(nx)]

    def hops(o):
        return sum(min(v, n - v) for v, n in zip(o, sizes))

    return sorted((o for o in every if o != (0, 0, 0)), key=lambda o: (-hops(o), o[1], o[2], o[0]))


def iota(shape, dim):
    return lax.broadcasted_iota(jnp.int32, shape, dim)


def one_hot(cond):
    return jnp.where(cond, 1.0, 0.0).astype(BF16)


def mm(a, b):
    return jnp.dot(a, b, preferred_element_type=F32)


def layer_norm(values, gain_row):
    center = values - jnp.mean(values, axis=1, keepdims=True)
    spread = jnp.mean(center * center, axis=1, keepdims=True)
    return center * lax.rsqrt(spread + 1e-05) * gain_row


def stack_halves(rows):
    return jnp.concatenate((rows[:, :HALF], rows[:, HALF:]), axis=0)


def join_halves(stacked):
    count = stacked.shape[0] // 2
    return jnp.concatenate((stacked[:count], stacked[count:]), axis=1)


def kernel(
    sizes, feat_hbm, orders_hbm, gains_hbm, qkv_hbm, proj_hbm, fc1_hbm, fc2_hbm, out_ref,
    feat, orders, gains, qkv_w, proj_w, fc1_w, fc2_w,
    req_send, req_recv, row_send, row_recv, near,
    pick_in, pick_back, pick_out, pick_home, spread, q_buf, k_buf, v_buf, score_a, score_b, totals, peaks, mixed,
    load_sem, self_sem, req_ssem, req_rsem, row_ssem, row_rsem, near_ssem, near_rsem,
):
    nz, ny, nx = sizes
    peers = nz * ny * nx
    rows = feat.shape[0]
    width = 2 * HALF
    slots = SLOTS * peers
    blocks = orders.shape[0]
    me = lax.axis_index("pts")
    zs = [jnp.bitwise_and(jnp.right_shift(me, 4) + i, nz - 1) * (ny * nx) for i in range(nz)]
    ys = [jnp.bitwise_and(jnp.right_shift(me, 2) + i, ny - 1) * nx for i in range(ny)]
    xs = [jnp.bitwise_and(me + i, nx - 1) for i in range(nx)]
    order = offsets(sizes)

    barrier = pltpu.get_barrier_semaphore()

    for a, b, c in order:
        other = zs[a] + ys[b] + xs[c]
        pl.semaphore_signal(barrier, inc=1, device_id={"pts": other}, device_id_type=MESH)

    loads = [
        pltpu.make_async_copy(src, dst, load_sem.at[i])
        for i, (src, dst) in enumerate(
            (
                (orders_hbm, orders), (feat_hbm, feat), (gains_hbm, gains), (qkv_hbm, qkv_w),
                (proj_hbm, proj_w), (fc1_hbm, fc1_w), (fc2_hbm, fc2_w),
            )
        )
    ]
    for load in loads:
        load.start()
    loads[0].wait()

    ri = iota((rows, rows), 0)
    ci = iota((rows, rows), 1)
    keys = []
    left, right = [], []
    for b in range(blocks):
        order_row = orders[b : b + 1, :]
        owner_row = jnp.right_shift(order_row, 8).astype(F32)
        within_row = jnp.bitwise_and(order_row, rows - 1).astype(F32)
        owner_col = jnp.sum(jnp.where(ri == ci, owner_row, 0.0), axis=1, keepdims=True)
        within_col = jnp.sum(jnp.where(ri == ci, within_row, 0.0), axis=1, keepdims=True)
        same = owner_col == owner_row
        rank_col = jnp.sum(jnp.where(same & (ci < ri), 1.0, 0.0), axis=1, keepdims=True)
        rank_row = jnp.sum(jnp.where(same & (ri < ci), 1.0, 0.0), axis=0, keepdims=True)
        keys.append(
            (
                (2.0 * (rank_row * peers + owner_row)).astype(jnp.int32),
                (2.0 * (rank_col * peers + owner_col)).astype(jnp.int32),
            )
        )
        left.append(one_hot(ri == (2.0 * owner_row + b).astype(jnp.int32)))
        lane = iota((rows, HALF), 1)
        right.append(
            jnp.where(rank_col.astype(jnp.int32) == lane, within_col + 1.0, 0.0).astype(BF16)
        )
    request = mm(jnp.concatenate(left, axis=1), jnp.concatenate(right, axis=0))
    req_send.reshape(2 * peers, HALF)[...] = request.astype(BF16)

    pl.semaphore_wait(barrier, peers - 1)

    def to_all(src, dst, ssem, rsem, mine):
        own = pltpu.make_async_copy(src(me), dst(me), mine)
        own.start()
        for a, b, c in order:
            other = zs[a] + ys[b] + xs[c]
            pltpu.make_async_remote_copy(
                src_ref=src(other), dst_ref=dst(me), send_sem=ssem, recv_sem=rsem,
                device_id={"pts": other}, device_id_type=MESH,
            ).start()
        own.wait()

    def all_of(ref, sem):
        pltpu.make_async_copy(ref, ref, sem).wait()

    to_all(lambda i: req_send.at[i], lambda i: req_recv.at[i], req_ssem, req_rsem, self_sem.at[0])

    for b in range(blocks):
        key_row, key_col = keys[b]
        for half in range(2):
            part = pl.ds(half * rows, rows)
            pick_in[b, part, :] = one_hot(iota((rows, 2 * slots), 1) == key_col + half)
            pick_back[b, :, part] = one_hot(iota((2 * slots, rows), 0) == key_row + half)
        spread[b] = one_hot(ri - jnp.bitwise_and(ri, 1) + b == ci)
    for load in loads[1:]:
        load.wait()

    q_buf[0 : 2 * rows, :HALF] = stack_halves(layer_norm(feat[...], gains[0, 0:1, :]).astype(BF16))
    all_of(req_recv.at[pl.ds(0, peers - 1)], req_rsem)
    asked = req_recv.reshape(2 * peers, HALF)[...]

    def selections(b):
        wanted = mm(spread[b], asked)
        parity = jnp.bitwise_and(iota(wanted.shape, 0), 1).astype(F32)
        wanted = jnp.where(wanted > 0.5, wanted - 1.0 + rows * parity, -4.0)
        return wanted

    def fill_out(b, wanted):
        for j in range(SLOTS):
            col = wanted[:, j : j + 1].astype(jnp.int32)
            pick_out[b, pl.ds(j * 2 * peers, 2 * peers), :] = one_hot(iota((2 * peers, 2 * rows), 1) == col)

    def fill_home(b, wanted):
        flat = wanted.T.astype(jnp.int32)
        for j in range(SLOTS):
            pick_home[b, :, pl.ds(j * 2 * peers, 2 * peers)] = one_hot(
                iota((2 * rows, 2 * peers), 0) == flat[j : j + 1, :]
            )

    def ship(phase, values):
        row_send.at[phase].reshape(2 * slots, HALF)[...] = values.astype(BF16)
        to_all(
            lambda i: row_send.at[phase, :, i], lambda i: row_recv.at[phase, :, i],
            row_ssem.at[phase], row_rsem.at[phase], self_sem.at[1 + phase],
        )

    def landed(phase):
        all_of(row_recv.at[phase, :, pl.ds(0, peers - 1)], row_rsem.at[phase])
        return row_recv.at[phase].reshape(2 * slots, HALF)[...]

    wanted0 = selections(0)
    fill_out(0, wanted0)
    ship(0, mm(pick_out[0], q_buf[0 : 2 * rows, :HALF]))

    fill_home(0, wanted0)
    wanted1 = selections(1)
    fill_out(1, wanted1)
    fill_home(1, wanted1)

    scale = (width // HEADS) ** (-0.5) * math.log2(math.e)
    half_rows = rows // 2
    top, bottom = pl.ds(0, half_rows), pl.ds(half_rows, half_rows)
    near_copies = []
    for b in range(blocks):
        near[b, 0] = join_halves(mm(pick_in[b], landed(2 * b))).astype(BF16)

        def pass_on(index, source, slot, part, step):
            copy = pltpu.make_async_remote_copy(
                src_ref=near.at[b, source, part], dst_ref=near.at[b, slot, part],
                send_sem=near_ssem.at[b, index], recv_sem=near_rsem.at[b, index],
                device_id={"pts": me - xs[0] + xs[step]}, device_id_type=MESH,
            )
            copy.start()
            near_copies.append(copy)
            return copy

        up_top = pass_on(0, 0, 1, top, 1)
        down_bottom = pass_on(1, 0, 3, bottom, 3)
        up_bottom = pass_on(2, 0, 1, bottom, 1)
        down_top = pass_on(3, 0, 3, top, 3)

        def keep(at, pair):
            k_buf[pl.ds(at * rows, rows), :] = pair[:, :width].astype(BF16)
            values = pair[:, width:].astype(BF16)
            ones = jnp.ones((rows, HALF), BF16)
            for half in range(2):
                v_buf[half, pl.ds(at * rows, rows), :] = jnp.concatenate(
                    (values[:, half * HALF : (half + 1) * HALF], ones), axis=1
                )

        def attend(at, first, last):
            keys = pl.ds(at * rows, rows)
            count = GROUP * rows

            def part_of(i):
                return pl.ds(pl.multiple_of(i * count, count), count)

            def score(i, into):
                into[...] = lax.dot_general(
                    q_buf[part_of(i), :], k_buf[keys, :], (((1,), (1,)), ((), ())),
                    preferred_element_type=F32,
                )

            def absorb(i, scores_ref):
                part = part_of(i)
                group = i * GROUP // (HEADS // 2)
                scores = scores_ref[...]
                low, high = scores[:, :HALF], scores[:, HALF:]
                peak = jnp.broadcast_to(
                    jnp.max(jnp.maximum(low, high), axis=1, keepdims=True), (count, HALF)
                )
                if not first:
                    before = peaks[part, :]
                    peak = jnp.maximum(before, peak)
                    decay = jnp.exp2(before - peak)
                if not last:
                    peaks[part, :] = peak
                weights = jnp.exp2(
                    jnp.concatenate(((low - peak).astype(BF16), (high - peak).astype(BF16)), axis=1)
                )
                both = mm(weights, v_buf[group, keys, :])
                tops, sums = both[:, :HALF], both[:, HALF:]
                if not first:
                    tops = tops + totals[part, :HALF] * decay
                    sums = sums + totals[part, HALF:] * decay
                if not last:
                    totals[part, :HALF] = tops
                    totals[part, HALF:] = sums
                else:
                    result = tops / sums
                    owner = jnp.right_shift(iota((rows, HALF), 1), 4)
                    within = GROUP * i % (HEADS // 2)
                    merged = mixed[group]
                    for g in range(GROUP):
                        merged = jnp.where(owner == within + g, result[g * rows : (g + 1) * rows], merged)
                    mixed[group] = merged

            steps = HEADS // GROUP
            score(0, score_a)

            def some(ii, carry):
                for u in range(0, UNROLL, 2):
                    i = ii * UNROLL + u
                    score(i + 1, score_b)
                    absorb(i, score_a)
                    score((i + 2) % steps, score_a)
                    absorb(i + 1, score_b)
                return carry

            lax.fori_loop(0, steps // UNROLL, some, 0)

        projected = mm(near[b, 0], qkv_w[b])
        queries = (projected[:, :width] * scale).astype(BF16)
        for h in range(HEADS):
            q_buf[pl.ds(h * rows, rows), :] = queries * one_hot(jnp.right_shift(iota((1, width), 1), 4) == h)
        keep(0, projected[:, width:])
        attend(0, True, False)

        up_top.wait_recv()
        far_top = pass_on(4, 1, 2, top, 1)
        down_bottom.wait_recv()
        far_bottom = pass_on(5, 3, 2, bottom, 3)
        def others(at, block):
            keep(at, mm(block, qkv_w[b, :, width:]))

        others(1, jnp.concatenate((near[b, 1, top], near[b, 3, bottom]), axis=0))
        attend(1, False, False)
        up_bottom.wait_recv()
        down_top.wait_recv()
        others(2, jnp.concatenate((near[b, 3, top], near[b, 1, bottom]), axis=0))
        attend(2, False, False)
        far_top.wait_recv()
        far_bottom.wait_recv()
        others(3, near[b, 2])
        attend(3, False, True)
        heads = jnp.concatenate((mixed[0], mixed[1]), axis=1).astype(BF16)
        branch = mm(heads, proj_w[b]).astype(BF16)
        ship(2 * b + 1, mm(pick_back[b], stack_halves(branch)))

        attended = feat[...] + join_halves(mm(pick_home[b], landed(2 * b + 1)))
        normed_two = layer_norm(attended, gains[b, 1:2, :]).astype(BF16)
        hidden = mm(normed_two, fc1_w[b])
        expanded = (0.5 * hidden * (1.0 + lax.erf(hidden * (0.5**0.5)))).astype(BF16)
        state = attended + mm(expanded, fc2_w[b])
        if b + 1 < blocks:
            normed = layer_norm(state, gains[b + 1, 0:1, :]).astype(BF16)
            ship(2 * b + 2, mm(pick_out[b + 1], stack_halves(normed)))
            feat[...] = state
        else:
            out_ref[...] = state

    all_of(req_send.at[pl.ds(0, peers - 1)], req_ssem)
    for phase in range(2 * blocks):
        all_of(row_send.at[phase, :, pl.ds(0, peers - 1)], row_ssem.at[phase])
    for copy in near_copies:
        copy.wait_send()


def local(sizes, features, orders, norm_gains, qkv_weight, proj_weight, fc1_weight, fc2_weight):
    rows, width = features.shape
    peers = math.prod(sizes)
    blocks = orders.shape[0]
    args = (features, orders, norm_gains, qkv_weight, proj_weight, fc1_weight, fc2_weight)
    slots = SLOTS * peers
    return pl.pallas_call(
        functools.partial(kernel, sizes),
        out_shape=jax.ShapeDtypeStruct((rows, width), F32),
        in_specs=[pl.BlockSpec(memory_space=pl.ANY)] * len(args),
        out_specs=pl.BlockSpec(memory_space=pltpu.VMEM),
        scratch_shapes=[pltpu.VMEM(a.shape, a.dtype) for a in args]
        + [
            pltpu.VMEM((peers, 2, HALF), BF16),
            pltpu.VMEM((peers, 2, HALF), BF16),
            pltpu.VMEM((2 * blocks, SLOTS, peers, 2, HALF), BF16),
            pltpu.VMEM((2 * blocks, SLOTS, peers, 2, HALF), BF16),
            pltpu.VMEM((blocks, PATCH // rows, rows, width), BF16),
            pltpu.VMEM((blocks, 2 * rows, 2 * slots), BF16),
            pltpu.VMEM((blocks, 2 * slots, 2 * rows), BF16),
            pltpu.VMEM((blocks, 2 * slots, 2 * rows), BF16),
            pltpu.VMEM((blocks, 2 * rows, 2 * slots), BF16),
            pltpu.VMEM((blocks, rows, rows), BF16),
            pltpu.VMEM((HEADS * rows, width), BF16),
            pltpu.VMEM((PATCH, width), BF16),
            pltpu.VMEM((2, PATCH, width), BF16),
            pltpu.VMEM((GROUP * rows, rows), F32),
            pltpu.VMEM((GROUP * rows, rows), F32),
            pltpu.VMEM((HEADS * rows, width), F32),
            pltpu.VMEM((HEADS * rows, HALF), F32),
            pltpu.VMEM((2, rows, HALF), F32),
            pltpu.SemaphoreType.DMA((len(args),)),
            pltpu.SemaphoreType.DMA((1 + 2 * blocks,)),
            pltpu.SemaphoreType.DMA,
            pltpu.SemaphoreType.DMA,
            pltpu.SemaphoreType.DMA((2 * blocks,)),
            pltpu.SemaphoreType.DMA((2 * blocks,)),
            pltpu.SemaphoreType.DMA((blocks, 6)),
            pltpu.SemaphoreType.DMA((blocks, 6)),
        ],
        compiler_params=pltpu.CompilerParams(collective_id=0, has_side_effects=True),
    )(*args)


def solution(mesh):
    sizes = (8, 4, 4)
    placed = (P(("slab", "pts"), None), P(None, ("slab", "pts")), P(), P(), P(), P(), P())
    return jax.shard_map(
        functools.partial(local, sizes),
        mesh=mesh,
        in_specs=placed,
        out_specs=P(("slab", "pts"), None),
        check_vma=False,
    )
```

```python
import functools
import math

import jax
import jax.numpy as jnp
from jax import lax
from jax.experimental import pallas as pl
from jax.experimental.pallas import tpu as pltpu
from jax.sharding import PartitionSpec as P

HEADS = 16
PATCH = 1024
HALF = 128
GROUP = 2
SLOTS = 3
F32 = jnp.float32
BF16 = jnp.bfloat16
MESH = pl.DeviceIdType.MESH


def offsets(sizes):
    nz, ny, nx = sizes
    every = [(a, b, c) for a in range(nz) for b in range(ny) for c in range(nx)]

    def hops(o):
        return sum(min(v, n - v) for v, n in zip(o, sizes))

    return sorted((o for o in every if o != (0, 0, 0)), key=lambda o: (-hops(o), o[1], o[2], o[0]))


def iota(shape, dim):
    return lax.broadcasted_iota(jnp.int32, shape, dim)


def one_hot(cond):
    return jnp.where(cond, 1.0, 0.0).astype(BF16)


def mm(a, b):
    return jnp.dot(a, b, preferred_element_type=F32)


def move_rows(picks, b, rows):
    count = picks.shape[1] // 2
    parts = [mm(picks[b, i * count : (i + 1) * count, :], rows) for i in range(2)]
    return jnp.concatenate(parts, axis=0)


def layer_norm(values, gain_row):
    center = values - jnp.mean(values, axis=1, keepdims=True)
    spread = jnp.mean(center * center, axis=1, keepdims=True)
    return center * lax.rsqrt(spread + 1e-05) * gain_row


def stack_halves(rows):
    return jnp.concatenate((rows[:, :HALF], rows[:, HALF:]), axis=0)


def join_halves(stacked):
    count = stacked.shape[0] // 2
    return jnp.concatenate((stacked[:count], stacked[count:]), axis=1)


def kernel(
    sizes, feat_hbm, orders_hbm, gains_hbm, qkv_hbm, proj_hbm, fc1_hbm, fc2_hbm, out_ref,
    feat, orders, gains, qkv_w, proj_w, fc1_w, fc2_w,
    req_send, req_recv, row_send, row_recv, near,
    pick_in, pick_back, pick_out, pick_home, spread, q_buf, k_buf, v_buf, score_a, score_b, totals, peaks, mixed,
    load_sem, self_sem, req_ssem, req_rsem, row_ssem, row_rsem, near_ssem, near_rsem,
):
    nz, ny, nx = sizes
    peers = nz * ny * nx
    rows = feat.shape[0]
    width = 2 * HALF
    slots = SLOTS * peers
    blocks = orders.shape[0]
    me = lax.axis_index("pts")
    zs = [jnp.bitwise_and(jnp.right_shift(me, 4) + i, nz - 1) * (ny * nx) for i in range(nz)]
    ys = [jnp.bitwise_and(jnp.right_shift(me, 2) + i, ny - 1) * nx for i in range(ny)]
    xs = [jnp.bitwise_and(me + i, nx - 1) for i in range(nx)]
    order = offsets(sizes)

    barrier = pltpu.get_barrier_semaphore()

    for a, b, c in order:
        other = zs[a] + ys[b] + xs[c]
        pl.semaphore_signal(barrier, inc=1, device_id={"pts": other}, device_id_type=MESH)

    loads = [
        pltpu.make_async_copy(src, dst, load_sem.at[i])
        for i, (src, dst) in enumerate(
            (
                (orders_hbm, orders), (feat_hbm, feat), (gains_hbm, gains), (qkv_hbm, qkv_w),
                (proj_hbm, proj_w), (fc1_hbm, fc1_w), (fc2_hbm, fc2_w),
            )
        )
    ]
    for load in loads:
        load.start()
    loads[0].wait()

    ri = iota((rows, rows), 0)
    ci = iota((rows, rows), 1)
    keys = []
    left, right = [], []
    for b in range(blocks):
        order_row = orders[b : b + 1, :]
        owner_row = jnp.right_shift(order_row, 8).astype(F32)
        within_row = jnp.bitwise_and(order_row, rows - 1).astype(F32)
        owner_col = jnp.sum(jnp.where(ri == ci, owner_row, 0.0), axis=1, keepdims=True)
        within_col = jnp.sum(jnp.where(ri == ci, within_row, 0.0), axis=1, keepdims=True)
        same = owner_col == owner_row
        rank_col = jnp.sum(jnp.where(same & (ci < ri), 1.0, 0.0), axis=1, keepdims=True)
        rank_row = jnp.sum(jnp.where(same & (ri < ci), 1.0, 0.0), axis=0, keepdims=True)
        keys.append(
            (
                (2.0 * (rank_row * peers + owner_row)).astype(jnp.int32),
                (2.0 * (rank_col * peers + owner_col)).astype(jnp.int32),
            )
        )
        left.append(one_hot(ri == (2.0 * owner_row + b).astype(jnp.int32)))
        lane = iota((rows, HALF), 1)
        right.append(
            jnp.where(rank_col.astype(jnp.int32) == lane, within_col + 1.0, 0.0).astype(BF16)
        )
    request = mm(jnp.concatenate(left, axis=1), jnp.concatenate(right, axis=0))
    req_send.reshape(2 * peers, HALF)[...] = request.astype(BF16)

    pl.semaphore_wait(barrier, peers - 1)

    def to_all(src, dst, ssem, rsem, mine):
        own = pltpu.make_async_copy(src(me), dst(me), mine)
        own.start()
        for a, b, c in order:
            other = zs[a] + ys[b] + xs[c]
            pltpu.make_async_remote_copy(
                src_ref=src(other), dst_ref=dst(me), send_sem=ssem, recv_sem=rsem,
                device_id={"pts": other}, device_id_type=MESH,
            ).start()
        own.wait()

    def all_of(ref, sem):
        pltpu.make_async_copy(ref, ref, sem).wait()

    to_all(lambda i: req_send.at[i], lambda i: req_recv.at[i], req_ssem, req_rsem, self_sem.at[0])

    for b in range(blocks):
        key_row, key_col = keys[b]
        for half in range(2):
            part = pl.ds(half * rows, rows)
            pick_in[b, part, :] = one_hot(iota((rows, 2 * slots), 1) == key_col + half)
            pick_back[b, :, part] = one_hot(iota((2 * slots, rows), 0) == key_row + half)
        spread[b] = one_hot(ri - jnp.bitwise_and(ri, 1) + b == ci)
    for load in loads[1:]:
        load.wait()

    q_buf[0 : 2 * rows, :] = stack_halves(layer_norm(feat[...], gains[0, 0:1, :]).astype(BF16))
    all_of(req_recv.at[pl.ds(0, peers - 1)], req_rsem)
    asked = req_recv.reshape(2 * peers, HALF)[...]

    def selections(b):
        wanted = mm(spread[b], asked)
        parity = jnp.bitwise_and(iota(wanted.shape, 0), 1).astype(F32)
        wanted = jnp.where(wanted > 0.5, wanted - 1.0 + rows * parity, -4.0)
        return wanted

    def fill_out(b, wanted):
        for j in range(SLOTS):
            col = wanted[:, j : j + 1].astype(jnp.int32)
            pick_out[b, pl.ds(j * 2 * peers, 2 * peers), :] = one_hot(iota((2 * peers, 2 * rows), 1) == col)

    def fill_home(b, wanted):
        flat = wanted.T.astype(jnp.int32)
        for j in range(SLOTS):
            pick_home[b, :, pl.ds(j * 2 * peers, 2 * peers)] = one_hot(
                iota((2 * rows, 2 * peers), 0) == flat[j : j + 1, :]
            )

    def ship(phase, values):
        row_send.at[phase].reshape(2 * slots, HALF)[...] = values.astype(BF16)
        to_all(
            lambda i: row_send.at[phase, :, i], lambda i: row_recv.at[phase, :, i],
            row_ssem.at[phase], row_rsem.at[phase], self_sem.at[1 + phase],
        )

    def landed(phase):
        all_of(row_recv.at[phase, :, pl.ds(0, peers - 1)], row_rsem.at[phase])
        return row_recv.at[phase].reshape(2 * slots, HALF)[...]

    wanted0 = selections(0)
    fill_out(0, wanted0)
    ship(0, move_rows(pick_out, 0, q_buf[0 : 2 * rows, :]))

    fill_home(0, wanted0)
    wanted1 = selections(1)
    fill_out(1, wanted1)
    fill_home(1, wanted1)

    scale = (width // HEADS) ** (-0.5) * math.log2(math.e)
    half_rows = rows // 2
    top, bottom = pl.ds(0, half_rows), pl.ds(half_rows, half_rows)
    near_copies = []
    for b in range(blocks):
        near[b, 0] = join_halves(move_rows(pick_in, b, landed(2 * b))).astype(BF16)

        def pass_on(index, source, slot, part, step):
            copy = pltpu.make_async_remote_copy(
                src_ref=near.at[b, source, part], dst_ref=near.at[b, slot, part],
                send_sem=near_ssem.at[b, index], recv_sem=near_rsem.at[b, index],
                device_id={"pts": me - xs[0] + xs[step]}, device_id_type=MESH,
            )
            copy.start()
            near_copies.append(copy)
            return copy

        up_top = pass_on(0, 0, 1, top, 1)
        down_bottom = pass_on(1, 0, 3, bottom, 3)
        up_bottom = pass_on(2, 0, 1, bottom, 1)
        down_top = pass_on(3, 0, 3, top, 3)

        def keep(at, pair):
            for half in range(2):
                k_buf[half, pl.ds(at * rows, rows), :] = pair[:, half * HALF : (half + 1) * HALF].astype(BF16)
            values = pair[:, width:].astype(BF16)
            ones = jnp.ones((rows, HALF), BF16)
            for half in range(2):
                v_buf[half, pl.ds(at * rows, rows), :] = jnp.concatenate(
                    (values[:, half * HALF : (half + 1) * HALF], ones), axis=1
                )

        def attend(at, first, last):
            keys = pl.ds(at * rows, rows)
            count = GROUP * rows

            def part_of(i):
                return pl.ds(i * count, count)

            def score(i, into):
                into[...] = lax.dot_general(
                    q_buf[part_of(i), :], k_buf[i * GROUP // (HEADS // 2), keys, :],
                    (((1,), (1,)), ((), ())), preferred_element_type=F32,
                )

            def absorb(i, scores_ref):
                part = part_of(i)
                group = i * GROUP // (HEADS // 2)
                scores = scores_ref[...]
                low, high = scores[:, :HALF], scores[:, HALF:]
                peak = jnp.broadcast_to(
                    jnp.max(jnp.maximum(low, high), axis=1, keepdims=True), (count, HALF)
                )
                if not first:
                    before = peaks[part, :]
                    peak = jnp.maximum(before, peak)
                    decay = jnp.exp2(before - peak)
                if not last:
                    peaks[part, :] = peak
                weights = jnp.exp2(
                    jnp.concatenate(((low - peak).astype(BF16), (high - peak).astype(BF16)), axis=1)
                )
                both = mm(weights, v_buf[group, keys, :])
                tops, sums = both[:, :HALF], both[:, HALF:]
                if not first:
                    tops = tops + totals[part, :HALF] * decay
                    sums = sums + totals[part, HALF:] * decay
                if not last:
                    totals[part, :HALF] = tops
                    totals[part, HALF:] = sums
                else:
                    result = tops / sums
                    owner = jnp.right_shift(iota((rows, HALF), 1), 4)
                    within = GROUP * i % (HEADS // 2)
                    merged = mixed[group]
                    for g in range(GROUP):
                        merged = jnp.where(owner == within + g, result[g * rows : (g + 1) * rows], merged)
                    mixed[group] = merged

            steps = HEADS // GROUP
            score(0, score_a)

            for i in range(0, steps, 2):
                score(i + 1, score_b)
                absorb(i, score_a)
                if i + 2 < steps:
                    score(i + 2, score_a)
                absorb(i + 1, score_b)

        projected = mm(near[b, 0], qkv_w[b])
        queries = (projected[:, :width] * scale).astype(BF16)
        for h in range(HEADS):
            half = h // (HEADS // 2)
            mask = one_hot(jnp.right_shift(iota((1, HALF), 1), 4) == h % (HEADS // 2))
            q_buf[pl.ds(h * rows, rows), :] = queries[:, half * HALF : (half + 1) * HALF] * mask
        keep(0, projected[:, width:])
        attend(0, True, False)

        up_top.wait_recv()
        far_top = pass_on(4, 1, 2, top, 1)
        down_bottom.wait_recv()
        far_bottom = pass_on(5, 3, 2, bottom, 3)
        def others(at, block):
            keep(at, mm(block, qkv_w[b, :, width:]))

        others(1, jnp.concatenate((near[b, 1, top], near[b, 3, bottom]), axis=0))
        attend(1, False, False)
        up_bottom.wait_recv()
        down_top.wait_recv()
        others(2, jnp.concatenate((near[b, 3, top], near[b, 1, bottom]), axis=0))
        attend(2, False, False)
        far_top.wait_recv()
        far_bottom.wait_recv()
        others(3, near[b, 2])
        attend(3, False, True)
        heads = jnp.concatenate((mixed[0], mixed[1]), axis=1).astype(BF16)
        branch = mm(heads, proj_w[b]).astype(BF16)
        ship(2 * b + 1, move_rows(pick_back, b, stack_halves(branch)))

        attended = feat[...] + join_halves(move_rows(pick_home, b, landed(2 * b + 1)))
        normed_two = layer_norm(attended, gains[b, 1:2, :]).astype(BF16)
        hidden = mm(normed_two, fc1_w[b])
        expanded = (0.5 * hidden * (1.0 + lax.erf(hidden * (0.5**0.5)))).astype(BF16)
        state = attended + mm(expanded, fc2_w[b])
        if b + 1 < blocks:
            normed = layer_norm(state, gains[b + 1, 0:1, :]).astype(BF16)
            ship(2 * b + 2, move_rows(pick_out, b + 1, stack_halves(normed)))
            feat[...] = state
        else:
            out_ref[...] = state

    all_of(req_send.at[pl.ds(0, peers - 1)], req_ssem)
    for phase in range(2 * blocks):
        all_of(row_send.at[phase, :, pl.ds(0, peers - 1)], row_ssem.at[phase])
    for copy in near_copies:
        copy.wait_send()


def local(sizes, features, orders, norm_gains, qkv_weight, proj_weight, fc1_weight, fc2_weight):
    rows, width = features.shape
    peers = math.prod(sizes)
    blocks = orders.shape[0]
    args = (features, orders, norm_gains, qkv_weight, proj_weight, fc1_weight, fc2_weight)
    slots = SLOTS * peers
    return pl.pallas_call(
        functools.partial(kernel, sizes),
        out_shape=jax.ShapeDtypeStruct((rows, width), F32),
        in_specs=[pl.BlockSpec(memory_space=pl.ANY)] * len(args),
        out_specs=pl.BlockSpec(memory_space=pltpu.VMEM),
        scratch_shapes=[pltpu.VMEM(a.shape, a.dtype) for a in args]
        + [
            pltpu.VMEM((peers, 2, HALF), BF16),
            pltpu.VMEM((peers, 2, HALF), BF16),
            pltpu.VMEM((2 * blocks, SLOTS, peers, 2, HALF), BF16),
            pltpu.VMEM((2 * blocks, SLOTS, peers, 2, HALF), BF16),
            pltpu.VMEM((blocks, PATCH // rows, rows, width), BF16),
            pltpu.VMEM((blocks, 2 * rows, 2 * slots), BF16),
            pltpu.VMEM((blocks, 2 * slots, 2 * rows), BF16),
            pltpu.VMEM((blocks, 2 * slots, 2 * rows), BF16),
            pltpu.VMEM((blocks, 2 * rows, 2 * slots), BF16),
            pltpu.VMEM((blocks, rows, rows), BF16),
            pltpu.VMEM((HEADS * rows, HALF), BF16),
            pltpu.VMEM((2, PATCH, HALF), BF16),
            pltpu.VMEM((2, PATCH, width), BF16),
            pltpu.VMEM((GROUP * rows, rows), F32),
            pltpu.VMEM((GROUP * rows, rows), F32),
            pltpu.VMEM((HEADS * rows, width), F32),
            pltpu.VMEM((HEADS * rows, HALF), F32),
            pltpu.VMEM((2, rows, HALF), F32),
            pltpu.SemaphoreType.DMA((len(args),)),
            pltpu.SemaphoreType.DMA((1 + 2 * blocks,)),
            pltpu.SemaphoreType.DMA,
            pltpu.SemaphoreType.DMA,
            pltpu.SemaphoreType.DMA((2 * blocks,)),
            pltpu.SemaphoreType.DMA((2 * blocks,)),
            pltpu.SemaphoreType.DMA((blocks, 6)),
            pltpu.SemaphoreType.DMA((blocks, 6)),
        ],
        compiler_params=pltpu.CompilerParams(collective_id=0, has_side_effects=True),
    )(*args)


def solution(mesh):
    sizes = (8, 4, 4)
    placed = (P(("slab", "pts"), None), P(None, ("slab", "pts")), P(), P(), P(), P(), P())
    return jax.shard_map(
        functools.partial(local, sizes),
        mesh=mesh,
        in_specs=placed,
        out_specs=P(("slab", "pts"), None),
        check_vma=False,
    )
```

```python
import functools
import math

import jax
import jax.numpy as jnp
from jax import lax
from jax.experimental import pallas as pl
from jax.experimental.pallas import tpu as pltpu
from jax.sharding import PartitionSpec as P

HEADS = 16
PATCH = 1024
HALF = 128
GROUP = 2
SLOTS = 3
F32 = jnp.float32
BF16 = jnp.bfloat16
MESH = pl.DeviceIdType.MESH


def offsets(sizes):
    nz, ny, nx = sizes
    every = [(a, b, c) for a in range(nz) for b in range(ny) for c in range(nx)]

    def hops(o):
        return sum(min(v, n - v) for v, n in zip(o, sizes))

    return sorted((o for o in every if o != (0, 0, 0)), key=lambda o: (-hops(o), o[1], o[2], o[0]))


def iota(shape, dim):
    return lax.broadcasted_iota(jnp.int32, shape, dim)


def one_hot(cond):
    return jnp.where(cond, 1.0, 0.0).astype(BF16)


def mm(a, b):
    return jnp.dot(a, b, preferred_element_type=F32)


def move_rows(picks, b, rows):
    count = picks.shape[1] // 2
    parts = [mm(picks[b, i * count : (i + 1) * count, :], rows) for i in range(2)]
    return jnp.concatenate(parts, axis=0)


def layer_norm(values, gain_row):
    center = values - jnp.mean(values, axis=1, keepdims=True)
    spread = jnp.mean(center * center, axis=1, keepdims=True)
    return center * lax.rsqrt(spread + 1e-05) * gain_row


def stack_halves(rows):
    return jnp.concatenate((rows[:, :HALF], rows[:, HALF:]), axis=0)


def join_halves(stacked):
    count = stacked.shape[0] // 2
    return jnp.concatenate((stacked[:count], stacked[count:]), axis=1)


def kernel(
    sizes, feat_hbm, orders_hbm, gains_hbm, qkv_hbm, proj_hbm, fc1_hbm, fc2_hbm, out_ref,
    feat, orders, gains, qkv_w, proj_w, fc1_w, fc2_w,
    req_send, req_recv, row_send, row_recv, near,
    pick_in, pick_back, pick_out, pick_home, spread, q_buf, k_buf, v_buf, score_a, score_b, totals, peaks, mixed,
    load_sem, self_sem, req_ssem, req_rsem, row_ssem, row_rsem, near_ssem, near_rsem,
):
    nz, ny, nx = sizes
    peers = nz * ny * nx
    rows = feat.shape[0]
    width = 2 * HALF
    slots = SLOTS * peers
    blocks = orders.shape[0]
    me = lax.axis_index("pts")
    zs = [jnp.bitwise_and(jnp.right_shift(me, 4) + i, nz - 1) * (ny * nx) for i in range(nz)]
    ys = [jnp.bitwise_and(jnp.right_shift(me, 2) + i, ny - 1) * nx for i in range(ny)]
    xs = [jnp.bitwise_and(me + i, nx - 1) for i in range(nx)]
    order = offsets(sizes)

    barrier = pltpu.get_barrier_semaphore()

    for a, b, c in order:
        other = zs[a] + ys[b] + xs[c]
        pl.semaphore_signal(barrier, inc=1, device_id={"pts": other}, device_id_type=MESH)

    loads = [
        pltpu.make_async_copy(src, dst, load_sem.at[i])
        for i, (src, dst) in enumerate(
            (
                (orders_hbm, orders), (feat_hbm, feat), (gains_hbm, gains), (qkv_hbm, qkv_w),
                (proj_hbm, proj_w), (fc1_hbm, fc1_w), (fc2_hbm, fc2_w),
            )
        )
    ]
    for load in loads:
        load.start()
    loads[0].wait()

    ri = iota((rows, rows), 0)
    ci = iota((rows, rows), 1)
    keys = []
    left, right = [], []
    for b in range(blocks):
        order_row = orders[b : b + 1, :]
        owner_row = jnp.right_shift(order_row, 8).astype(F32)
        within_row = jnp.bitwise_and(order_row, rows - 1).astype(F32)
        owner_col = jnp.sum(jnp.where(ri == ci, owner_row, 0.0), axis=1, keepdims=True)
        within_col = jnp.sum(jnp.where(ri == ci, within_row, 0.0), axis=1, keepdims=True)
        same = owner_col == owner_row
        rank_col = jnp.sum(jnp.where(same & (ci < ri), 1.0, 0.0), axis=1, keepdims=True)
        rank_row = jnp.sum(jnp.where(same & (ri < ci), 1.0, 0.0), axis=0, keepdims=True)
        keys.append(
            (
                (2.0 * (rank_row * peers + owner_row)).astype(jnp.int32),
                (2.0 * (rank_col * peers + owner_col)).astype(jnp.int32),
            )
        )
        left.append(one_hot(ri == (2.0 * owner_row + b).astype(jnp.int32)))
        lane = iota((rows, HALF), 1)
        right.append(
            jnp.where(rank_col.astype(jnp.int32) == lane, within_col + 1.0, 0.0).astype(BF16)
        )
    request = mm(jnp.concatenate(left, axis=1), jnp.concatenate(right, axis=0))
    req_send.reshape(2 * peers, HALF)[...] = request.astype(BF16)

    pl.semaphore_wait(barrier, peers - 1)

    def to_all(src, dst, ssem, rsem, mine):
        own = pltpu.make_async_copy(src(me), dst(me), mine)
        own.start()
        for a, b, c in order:
            other = zs[a] + ys[b] + xs[c]
            pltpu.make_async_remote_copy(
                src_ref=src(other), dst_ref=dst(me), send_sem=ssem, recv_sem=rsem,
                device_id={"pts": other}, device_id_type=MESH,
            ).start()
        own.wait()

    def all_of(ref, sem):
        pltpu.make_async_copy(ref, ref, sem).wait()

    to_all(lambda i: req_send.at[i], lambda i: req_recv.at[i], req_ssem, req_rsem, self_sem.at[0])

    for b in range(blocks):
        key_row, key_col = keys[b]
        for half in range(2):
            part = pl.ds(half * rows, rows)
            pick_in[b, part, :] = one_hot(iota((rows, 2 * slots), 1) == key_col + half)
            pick_back[b, :, part] = one_hot(iota((2 * slots, rows), 0) == key_row + half)
        spread[b] = one_hot(ri - jnp.bitwise_and(ri, 1) + b == ci)
    for load in loads[1:]:
        load.wait()

    q_buf[0 : 2 * rows, :] = stack_halves(layer_norm(feat[...], gains[0, 0:1, :]).astype(BF16))
    all_of(req_recv.at[pl.ds(0, peers - 1)], req_rsem)
    asked = req_recv.reshape(2 * peers, HALF)[...]

    def selections(b):
        wanted = mm(spread[b], asked)
        parity = jnp.bitwise_and(iota(wanted.shape, 0), 1).astype(F32)
        wanted = jnp.where(wanted > 0.5, wanted - 1.0 + rows * parity, -4.0)
        return wanted

    def fill_out(b, wanted):
        for j in range(SLOTS):
            col = wanted[:, j : j + 1].astype(jnp.int32)
            pick_out[b, pl.ds(j * 2 * peers, 2 * peers), :] = one_hot(iota((2 * peers, 2 * rows), 1) == col)

    def fill_home(b, wanted):
        flat = wanted.T.astype(jnp.int32)
        for j in range(SLOTS):
            pick_home[b, :, pl.ds(j * 2 * peers, 2 * peers)] = one_hot(
                iota((2 * rows, 2 * peers), 0) == flat[j : j + 1, :]
            )

    def ship(phase, values):
        row_send.at[phase].reshape(2 * slots, HALF)[...] = values.astype(BF16)
        to_all(
            lambda i: row_send.at[phase, :, i], lambda i: row_recv.at[phase, :, i],
            row_ssem.at[phase], row_rsem.at[phase], self_sem.at[1 + phase],
        )

    def landed(phase):
        all_of(row_recv.at[phase, :, pl.ds(0, peers - 1)], row_rsem.at[phase])
        return row_recv.at[phase].reshape(2 * slots, HALF)[...]

    wanted0 = selections(0)
    fill_out(0, wanted0)
    ship(0, move_rows(pick_out, 0, q_buf[0 : 2 * rows, :]))

    fill_home(0, wanted0)
    wanted1 = selections(1)
    fill_out(1, wanted1)
    fill_home(1, wanted1)

    scale = (width // HEADS) ** (-0.5) * math.log2(math.e)
    direct = rows * 5 // 8
    top, bottom = pl.ds(0, direct), pl.ds(direct, rows - direct)
    near_copies = []
    for b in range(blocks):
        near[b, 0] = join_halves(move_rows(pick_in, b, landed(2 * b))).astype(BF16)

        def pass_on(index, source, slot, part, step):
            copy = pltpu.make_async_remote_copy(
                src_ref=near.at[b, source, part], dst_ref=near.at[b, slot, part],
                send_sem=near_ssem.at[b, index], recv_sem=near_rsem.at[b, index],
                device_id={"pts": me - xs[0] + xs[step]}, device_id_type=MESH,
            )
            copy.start()
            near_copies.append(copy)
            return copy

        down_bottom = pass_on(1, 0, 3, bottom, 3)
        up_top = pass_on(0, 0, 1, top, 1)
        up_bottom = pass_on(2, 0, 1, bottom, 1)
        far_top = pass_on(4, 0, 2, top, 2)
        down_top = pass_on(3, 0, 3, top, 3)

        def keep(at, pair):
            for half in range(2):
                k_buf[half, pl.ds(at * rows, rows), :] = pair[:, half * HALF : (half + 1) * HALF].astype(BF16)
            values = pair[:, width:].astype(BF16)
            ones = jnp.ones((rows, HALF), BF16)
            for half in range(2):
                v_buf[half, pl.ds(at * rows, rows), :] = jnp.concatenate(
                    (values[:, half * HALF : (half + 1) * HALF], ones), axis=1
                )

        def attend(at, first, last):
            keys = pl.ds(at * rows, rows)
            count = GROUP * rows

            def part_of(i):
                return pl.ds(i * count, count)

            def score(i, into):
                into[...] = lax.dot_general(
                    q_buf[part_of(i), :], k_buf[i * GROUP // (HEADS // 2), keys, :],
                    (((1,), (1,)), ((), ())), preferred_element_type=F32,
                )

            def absorb(i, scores_ref):
                part = part_of(i)
                group = i * GROUP // (HEADS // 2)
                scores = scores_ref[...]
                low, high = scores[:, :HALF], scores[:, HALF:]
                peak = jnp.broadcast_to(
                    jnp.max(jnp.maximum(low, high), axis=1, keepdims=True), (count, HALF)
                )
                if not first:
                    before = peaks[part, :]
                    peak = jnp.maximum(before, peak)
                    decay = jnp.exp2(before - peak)
                if not last:
                    peaks[part, :] = peak
                weights = jnp.exp2(
                    jnp.concatenate(((low - peak).astype(BF16), (high - peak).astype(BF16)), axis=1)
                )
                both = mm(weights, v_buf[group, keys, :])
                tops, sums = both[:, :HALF], both[:, HALF:]
                if not first:
                    tops = tops + totals[part, :HALF] * decay
                    sums = sums + totals[part, HALF:] * decay
                if not last:
                    totals[part, :HALF] = tops
                    totals[part, HALF:] = sums
                else:
                    result = tops / sums
                    owner = jnp.right_shift(iota((rows, HALF), 1), 4)
                    within = GROUP * i % (HEADS // 2)
                    merged = mixed[group]
                    for g in range(GROUP):
                        merged = jnp.where(owner == within + g, result[g * rows : (g + 1) * rows], merged)
                    mixed[group] = merged

            steps = HEADS // GROUP
            score(0, score_a)

            for i in range(0, steps, 2):
                score(i + 1, score_b)
                absorb(i, score_a)
                if i + 2 < steps:
                    score(i + 2, score_a)
                absorb(i + 1, score_b)

        projected = mm(near[b, 0], qkv_w[b])
        queries = (projected[:, :width] * scale).astype(BF16)
        for h in range(HEADS):
            half = h // (HEADS // 2)
            mask = one_hot(jnp.right_shift(iota((1, HALF), 1), 4) == h % (HEADS // 2))
            q_buf[pl.ds(h * rows, rows), :] = queries[:, half * HALF : (half + 1) * HALF] * mask
        keep(0, projected[:, width:])
        attend(0, True, False)

        down_bottom.wait_recv()
        far_bottom = pass_on(5, 3, 2, bottom, 3)
        up_top.wait_recv()
        def others(at, block):
            keep(at, mm(block, qkv_w[b, :, width:]))

        others(1, jnp.concatenate((near[b, 1, top], near[b, 3, bottom]), axis=0))
        attend(1, False, False)
        up_bottom.wait_recv()
        down_top.wait_recv()
        others(2, jnp.concatenate((near[b, 3, top], near[b, 1, bottom]), axis=0))
        attend(2, False, False)
        far_top.wait_recv()
        far_bottom.wait_recv()
        others(3, near[b, 2])
        attend(3, False, True)
        heads = jnp.concatenate((mixed[0], mixed[1]), axis=1).astype(BF16)
        branch = mm(heads, proj_w[b]).astype(BF16)
        ship(2 * b + 1, move_rows(pick_back, b, stack_halves(branch)))

        attended = feat[...] + join_halves(move_rows(pick_home, b, landed(2 * b + 1)))
        normed_two = layer_norm(attended, gains[b, 1:2, :]).astype(BF16)
        hidden = mm(normed_two, fc1_w[b])
        expanded = (0.5 * hidden * (1.0 + lax.erf(hidden * (0.5**0.5)))).astype(BF16)
        state = attended + mm(expanded, fc2_w[b])
        if b + 1 < blocks:
            normed = layer_norm(state, gains[b + 1, 0:1, :]).astype(BF16)
            ship(2 * b + 2, move_rows(pick_out, b + 1, stack_halves(normed)))
            feat[...] = state
        else:
            out_ref[...] = state

    all_of(req_send.at[pl.ds(0, peers - 1)], req_ssem)
    for phase in range(2 * blocks):
        all_of(row_send.at[phase, :, pl.ds(0, peers - 1)], row_ssem.at[phase])
    for copy in near_copies:
        copy.wait_send()


def local(sizes, features, orders, norm_gains, qkv_weight, proj_weight, fc1_weight, fc2_weight):
    rows, width = features.shape
    peers = math.prod(sizes)
    blocks = orders.shape[0]
    args = (features, orders, norm_gains, qkv_weight, proj_weight, fc1_weight, fc2_weight)
    slots = SLOTS * peers
    return pl.pallas_call(
        functools.partial(kernel, sizes),
        out_shape=pltpu.VMEM((rows, width), F32),
        in_specs=[pl.BlockSpec(memory_space=pl.ANY)] * len(args),
        out_specs=pl.BlockSpec(memory_space=pltpu.VMEM),
        scratch_shapes=[pltpu.VMEM(a.shape, a.dtype) for a in args]
        + [
            pltpu.VMEM((peers, 2, HALF), BF16),
            pltpu.VMEM((peers, 2, HALF), BF16),
            pltpu.VMEM((2 * blocks, SLOTS, peers, 2, HALF), BF16),
            pltpu.VMEM((2 * blocks, SLOTS, peers, 2, HALF), BF16),
            pltpu.VMEM((blocks, PATCH // rows, rows, width), BF16),
            pltpu.VMEM((blocks, 2 * rows, 2 * slots), BF16),
            pltpu.VMEM((blocks, 2 * slots, 2 * rows), BF16),
            pltpu.VMEM((blocks, 2 * slots, 2 * rows), BF16),
            pltpu.VMEM((blocks, 2 * rows, 2 * slots), BF16),
            pltpu.VMEM((blocks, rows, rows), BF16),
            pltpu.VMEM((HEADS * rows, HALF), BF16),
            pltpu.VMEM((2, PATCH, HALF), BF16),
            pltpu.VMEM((2, PATCH, width), BF16),
            pltpu.VMEM((GROUP * rows, rows), F32),
            pltpu.VMEM((GROUP * rows, rows), F32),
            pltpu.VMEM((HEADS * rows, width), F32),
            pltpu.VMEM((HEADS * rows, HALF), F32),
            pltpu.VMEM((2, rows, HALF), F32),
            pltpu.SemaphoreType.DMA((len(args),)),
            pltpu.SemaphoreType.DMA((1 + 2 * blocks,)),
            pltpu.SemaphoreType.DMA,
            pltpu.SemaphoreType.DMA,
            pltpu.SemaphoreType.DMA((2 * blocks,)),
            pltpu.SemaphoreType.DMA((2 * blocks,)),
            pltpu.SemaphoreType.DMA((blocks, 6)),
            pltpu.SemaphoreType.DMA((blocks, 6)),
        ],
        compiler_params=pltpu.CompilerParams(collective_id=0, has_side_effects=True),
    )(*args)


def solution(mesh):
    sizes = (8, 4, 4)
    placed = (P(("slab", "pts"), None), P(None, ("slab", "pts")), P(), P(), P(), P(), P())
    return jax.shard_map(
        functools.partial(local, sizes),
        mesh=mesh,
        in_specs=placed,
        out_specs=P(("slab", "pts"), None),
        check_vma=False,
    )
```

```python
import functools
import math

import jax
import jax.numpy as jnp
from jax import lax
from jax.experimental import pallas as pl
from jax.experimental.pallas import tpu as pltpu
from jax.sharding import PartitionSpec as P

HEADS = 16
PATCH = 1024
HALF = 128
GROUP = 2
SLOTS = 3
F32 = jnp.float32
BF16 = jnp.bfloat16
MESH = pl.DeviceIdType.MESH


def offsets(sizes):
    nz, ny, nx = sizes
    every = [(a, b, c) for a in range(nz) for b in range(ny) for c in range(nx)]

    def hops(o):
        return sum(min(v, n - v) for v, n in zip(o, sizes))

    return sorted((o for o in every if o != (0, 0, 0)), key=lambda o: (-hops(o), o[1], o[2], o[0]))


def iota(shape, dim):
    return lax.broadcasted_iota(jnp.int32, shape, dim)


def one_hot(cond):
    return jnp.where(cond, 1.0, 0.0).astype(BF16)


def mm(a, b):
    return jnp.dot(a, b, preferred_element_type=F32)


def move_rows(picks, b, rows):
    count = picks.shape[1] // 2
    parts = [mm(picks[b, i * count : (i + 1) * count, :], rows) for i in range(2)]
    return jnp.concatenate(parts, axis=0)


def layer_norm(values, gain_row):
    center = values - jnp.mean(values, axis=1, keepdims=True)
    spread = jnp.mean(center * center, axis=1, keepdims=True)
    return center * lax.rsqrt(spread + 1e-05) * gain_row


def stack_halves(rows):
    return jnp.concatenate((rows[:, :HALF], rows[:, HALF:]), axis=0)


def join_halves(stacked):
    count = stacked.shape[0] // 2
    return jnp.concatenate((stacked[:count], stacked[count:]), axis=1)


def kernel(
    sizes, feat_hbm, orders_hbm, gains_hbm, qkv_hbm, proj_hbm, fc1_hbm, fc2_hbm, out_ref,
    feat, orders, gains, qkv_w, proj_w, fc1_w, fc2_w,
    req_send, req_recv, row_send, row_recv, near,
    pick_in, pick_back, pick_out, pick_home, spread, q_buf, k_buf, v_buf, score_a, score_b, totals, peaks, mixed,
    load_sem, self_sem, req_ssem, req_rsem, row_ssem, row_rsem, near_ssem, near_rsem,
):
    nz, ny, nx = sizes
    peers = nz * ny * nx
    rows = feat.shape[0]
    width = 2 * HALF
    slots = SLOTS * peers
    blocks = orders.shape[0]
    me = lax.axis_index("pts")
    zs = [jnp.bitwise_and(jnp.right_shift(me, 4) + i, nz - 1) * (ny * nx) for i in range(nz)]
    ys = [jnp.bitwise_and(jnp.right_shift(me, 2) + i, ny - 1) * nx for i in range(ny)]
    xs = [jnp.bitwise_and(me + i, nx - 1) for i in range(nx)]
    order = offsets(sizes)

    barrier = pltpu.get_barrier_semaphore()

    for a, b, c in order:
        other = zs[a] + ys[b] + xs[c]
        pl.semaphore_signal(barrier, inc=1, device_id={"pts": other}, device_id_type=MESH)

    loads = [
        pltpu.make_async_copy(src, dst, load_sem.at[i])
        for i, (src, dst) in enumerate(
            (
                (orders_hbm, orders), (feat_hbm, feat), (gains_hbm, gains), (qkv_hbm, qkv_w),
                (proj_hbm, proj_w), (fc1_hbm, fc1_w), (fc2_hbm, fc2_w),
            )
        )
    ]
    for load in loads:
        load.start()
    loads[0].wait()

    ri = iota((rows, rows), 0)
    ci = iota((rows, rows), 1)
    keys = []
    left, right = [], []
    for b in range(blocks):
        order_row = orders[b : b + 1, :]
        owner_row = jnp.right_shift(order_row, 8).astype(F32)
        within_row = jnp.bitwise_and(order_row, rows - 1).astype(F32)
        owner_col = jnp.sum(jnp.where(ri == ci, owner_row, 0.0), axis=1, keepdims=True)
        within_col = jnp.sum(jnp.where(ri == ci, within_row, 0.0), axis=1, keepdims=True)
        same = owner_col == owner_row
        rank_col = jnp.sum(jnp.where(same & (ci < ri), 1.0, 0.0), axis=1, keepdims=True)
        rank_row = jnp.sum(jnp.where(same & (ri < ci), 1.0, 0.0), axis=0, keepdims=True)
        keys.append(
            (
                (2.0 * (rank_row * peers + owner_row)).astype(jnp.int32),
                (2.0 * (rank_col * peers + owner_col)).astype(jnp.int32),
            )
        )
        left.append(one_hot(ri == (2.0 * owner_row + b).astype(jnp.int32)))
        lane = iota((rows, HALF), 1)
        right.append(
            jnp.where(rank_col.astype(jnp.int32) == lane, within_col + 1.0, 0.0).astype(BF16)
        )
    request = mm(jnp.concatenate(left, axis=1), jnp.concatenate(right, axis=0))
    req_send.reshape(2 * peers, HALF)[...] = request.astype(BF16)

    pl.semaphore_wait(barrier, peers - 1)

    def to_all(src, dst, ssem, rsem, mine):
        own = pltpu.make_async_copy(src(me), dst(me), mine)
        own.start()
        for a, b, c in order:
            other = zs[a] + ys[b] + xs[c]
            pltpu.make_async_remote_copy(
                src_ref=src(other), dst_ref=dst(me), send_sem=ssem, recv_sem=rsem,
                device_id={"pts": other}, device_id_type=MESH,
            ).start()
        own.wait()

    def all_of(ref, sem):
        pltpu.make_async_copy(ref, ref, sem).wait()

    to_all(lambda i: req_send.at[i], lambda i: req_recv.at[i], req_ssem, req_rsem, self_sem)

    for b in range(blocks):
        key_row, key_col = keys[b]
        for half in range(2):
            part = pl.ds(half * rows, rows)
            pick_in[b, part, :] = one_hot(iota((rows, 2 * slots), 1) == key_col + half)
            pick_back[b, :, part] = one_hot(iota((2 * slots, rows), 0) == key_row + half)
        spread[b] = one_hot(ri - jnp.bitwise_and(ri, 1) + b == ci)
    for load in loads[1:]:
        load.wait()

    q_buf[0 : 2 * rows, :] = stack_halves(layer_norm(feat[...], gains[0, 0:1, :]).astype(BF16))
    all_of(req_recv.at[pl.ds(0, peers - 1)], req_rsem)
    asked = req_recv.reshape(2 * peers, HALF)[...]

    def selections(b):
        wanted = mm(spread[b], asked)
        parity = jnp.bitwise_and(iota(wanted.shape, 0), 1).astype(F32)
        wanted = jnp.where(wanted > 0.5, wanted - 1.0 + rows * parity, -4.0)
        return wanted

    def fill_out(b, wanted):
        for j in range(SLOTS):
            col = wanted[:, j : j + 1].astype(jnp.int32)
            pick_out[b, pl.ds(j * 2 * peers, 2 * peers), :] = one_hot(iota((2 * peers, 2 * rows), 1) == col)

    def fill_home(b, wanted):
        flat = wanted.T.astype(jnp.int32)
        for j in range(SLOTS):
            pick_home[b, :, pl.ds(j * 2 * peers, 2 * peers)] = one_hot(
                iota((2 * rows, 2 * peers), 0) == flat[j : j + 1, :]
            )

    def ship(phase, values):
        row_send.at[phase].reshape(2 * slots, HALF)[...] = values.astype(BF16)
        to_all(
            lambda i: row_send.at[phase, :, i], lambda i: row_recv.at[phase, :, i],
            row_ssem, row_rsem.at[phase], self_sem,
        )

    def landed(phase):
        all_of(row_recv.at[phase, :, pl.ds(0, peers - 1)], row_rsem.at[phase])
        return row_recv.at[phase].reshape(2 * slots, HALF)[...]

    wanted0 = selections(0)
    fill_out(0, wanted0)
    ship(0, move_rows(pick_out, 0, q_buf[0 : 2 * rows, :]))

    fill_home(0, wanted0)
    wanted1 = selections(1)
    fill_out(1, wanted1)
    fill_home(1, wanted1)

    scale = (width // HEADS) ** (-0.5) * math.log2(math.e)
    direct = rows * 3 // 4
    top, bottom = pl.ds(0, direct), pl.ds(direct, rows - direct)
    for b in range(blocks):
        near[b, 0] = join_halves(move_rows(pick_in, b, landed(2 * b))).astype(BF16)

        def pass_on(index, source, slot, part, step):
            copy = pltpu.make_async_remote_copy(
                src_ref=near.at[b, source, part], dst_ref=near.at[b, slot, part],
                send_sem=near_ssem, recv_sem=near_rsem.at[b, index],
                device_id={"pts": me - xs[0] + xs[step]}, device_id_type=MESH,
            )
            copy.start()
            return copy

        down_bottom = pass_on(1, 0, 3, bottom, 3)
        up_top = pass_on(0, 0, 1, top, 1)
        up_bottom = pass_on(2, 0, 1, bottom, 1)
        far_top = pass_on(4, 0, 2, top, 2)
        down_top = pass_on(3, 0, 3, top, 3)

        def keep(at, pair, start=0):
            part = pl.ds(at * rows + start, pair.shape[0])
            for half in range(2):
                k_buf[half, part, :] = pair[:, half * HALF : (half + 1) * HALF].astype(BF16)
            values = pair[:, width:].astype(BF16)
            ones = jnp.ones((pair.shape[0], HALF), BF16)
            for half in range(2):
                v_buf[half, part, :] = jnp.concatenate(
                    (values[:, half * HALF : (half + 1) * HALF], ones), axis=1
                )

        def attend(at, first, last):
            keys = pl.ds(at * rows, rows)
            count = GROUP * rows

            def part_of(i):
                return pl.ds(i * count, count)

            def score(i, into):
                into[...] = lax.dot_general(
                    q_buf[part_of(i), :], k_buf[i * GROUP // (HEADS // 2), keys, :],
                    (((1,), (1,)), ((), ())), preferred_element_type=F32,
                )

            def absorb(i, scores_ref):
                part = part_of(i)
                group = i * GROUP // (HEADS // 2)
                scores = scores_ref[...]
                low, high = scores[:, :HALF], scores[:, HALF:]
                peak = jnp.broadcast_to(
                    jnp.max(jnp.maximum(low, high), axis=1, keepdims=True), (count, HALF)
                )
                if not first:
                    before = peaks[part, :]
                    peak = jnp.maximum(before, peak)
                    decay = jnp.exp2(before - peak)
                if not last:
                    peaks[part, :] = peak
                weights = jnp.exp2(
                    jnp.concatenate(((low - peak).astype(BF16), (high - peak).astype(BF16)), axis=1)
                )
                both = mm(weights, v_buf[group, keys, :])
                tops, sums = both[:, :HALF], both[:, HALF:]
                if not first:
                    tops = tops + totals[part, :HALF] * decay
                    sums = sums + totals[part, HALF:] * decay
                if not last:
                    totals[part, :HALF] = tops
                    totals[part, HALF:] = sums
                else:
                    result = tops / sums
                    owner = jnp.right_shift(iota((rows, HALF), 1), 4)
                    within = GROUP * i % (HEADS // 2)
                    merged = mixed[group]
                    for g in range(GROUP):
                        merged = jnp.where(owner == within + g, result[g * rows : (g + 1) * rows], merged)
                    mixed[group] = merged

            steps = HEADS // GROUP
            score(0, score_a)

            for i in range(0, steps, 2):
                score(i + 1, score_b)
                absorb(i, score_a)
                if i + 2 < steps:
                    score(i + 2, score_a)
                absorb(i + 1, score_b)

        projected = mm(near[b, 0], qkv_w[b])
        queries = (projected[:, :width] * scale).astype(BF16)
        for h in range(HEADS):
            half = h // (HEADS // 2)
            mask = one_hot(jnp.right_shift(iota((1, HALF), 1), 4) == h % (HEADS // 2))
            q_buf[pl.ds(h * rows, rows), :] = queries[:, half * HALF : (half + 1) * HALF] * mask
        keep(0, projected[:, width:])
        attend(0, True, False)

        down_bottom.wait_recv()
        far_bottom = pass_on(5, 3, 2, bottom, 3)
        up_top.wait_recv()
        def others(at, block, start=0):
            keep(at, mm(block, qkv_w[b, :, width:]), start)

        others(1, jnp.concatenate((near[b, 1, top], near[b, 3, bottom]), axis=0))
        attend(1, False, False)
        up_bottom.wait_recv()
        down_top.wait_recv()
        others(2, jnp.concatenate((near[b, 3, top], near[b, 1, bottom]), axis=0))
        attend(2, False, False)
        far_top.wait_recv()
        others(3, near[b, 2, top])
        far_bottom.wait_recv()
        others(3, near[b, 2, bottom], direct)
        attend(3, False, True)
        heads = jnp.concatenate((mixed[0], mixed[1]), axis=1).astype(BF16)
        branch = mm(heads, proj_w[b]).astype(BF16)
        ship(2 * b + 1, move_rows(pick_back, b, stack_halves(branch)))

        attended = feat[...] + join_halves(move_rows(pick_home, b, landed(2 * b + 1)))
        normed_two = layer_norm(attended, gains[b, 1:2, :]).astype(BF16)
        hidden = mm(normed_two, fc1_w[b])
        expanded = (0.5 * hidden * (1.0 + lax.erf(hidden * (0.5**0.5)))).astype(BF16)
        state = attended + mm(expanded, fc2_w[b])
        if b + 1 < blocks:
            normed = layer_norm(state, gains[b + 1, 0:1, :]).astype(BF16)
            ship(2 * b + 2, move_rows(pick_out, b + 1, stack_halves(normed)))
            feat[...] = state
        else:
            out_ref[...] = state

    all_of(req_send.at[pl.ds(0, peers - 1)], req_ssem)
    all_of(row_send.at[:, :, pl.ds(0, peers - 1)], row_ssem)
    all_of(near.at[:, pl.ds(0, PATCH // rows - 1)], near_ssem)


def local(sizes, features, orders, norm_gains, qkv_weight, proj_weight, fc1_weight, fc2_weight):
    rows, width = features.shape
    peers = math.prod(sizes)
    blocks = orders.shape[0]
    args = (features, orders, norm_gains, qkv_weight, proj_weight, fc1_weight, fc2_weight)
    slots = SLOTS * peers
    return pl.pallas_call(
        functools.partial(kernel, sizes),
        out_shape=pltpu.VMEM((rows, width), F32),
        in_specs=[pl.BlockSpec(memory_space=pl.ANY)] * len(args),
        out_specs=pl.BlockSpec(memory_space=pltpu.VMEM),
        scratch_shapes=[pltpu.VMEM(a.shape, a.dtype) for a in args]
        + [
            pltpu.VMEM((peers, 2, HALF), BF16),
            pltpu.VMEM((peers, 2, HALF), BF16),
            pltpu.VMEM((2 * blocks, SLOTS, peers, 2, HALF), BF16),
            pltpu.VMEM((2 * blocks, SLOTS, peers, 2, HALF), BF16),
            pltpu.VMEM((blocks, PATCH // rows, rows, width), BF16),
            pltpu.VMEM((blocks, 2 * rows, 2 * slots), BF16),
            pltpu.VMEM((blocks, 2 * slots, 2 * rows), BF16),
            pltpu.VMEM((blocks, 2 * slots, 2 * rows), BF16),
            pltpu.VMEM((blocks, 2 * rows, 2 * slots), BF16),
            pltpu.VMEM((blocks, rows, rows), BF16),
            pltpu.VMEM((HEADS * rows, HALF), BF16),
            pltpu.VMEM((2, PATCH, HALF), BF16),
            pltpu.VMEM((2, PATCH, width), BF16),
            pltpu.VMEM((GROUP * rows, rows), F32),
            pltpu.VMEM((GROUP * rows, rows), F32),
            pltpu.VMEM((HEADS * rows, width), F32),
            pltpu.VMEM((HEADS * rows, HALF), F32),
            pltpu.VMEM((2, rows, HALF), F32),
            pltpu.SemaphoreType.DMA((len(args),)),
            pltpu.SemaphoreType.DMA,
            pltpu.SemaphoreType.DMA,
            pltpu.SemaphoreType.DMA,
            pltpu.SemaphoreType.DMA,
            pltpu.SemaphoreType.DMA((2 * blocks,)),
            pltpu.SemaphoreType.DMA,
            pltpu.SemaphoreType.DMA((blocks, 6)),
        ],
        compiler_params=pltpu.CompilerParams(collective_id=0, has_side_effects=True),
    )(*args)


def solution(mesh):
    sizes = (8, 4, 4)
    placed = (P(("slab", "pts"), None), P(None, ("slab", "pts")), P(), P(), P(), P(), P())
    return jax.shard_map(
        functools.partial(local, sizes),
        mesh=mesh,
        in_specs=placed,
        out_specs=P(("slab", "pts"), None),
        check_vma=False,
    )
```
